32 devices in a mesh: row: 8 (over z, core), col: 4 (over y, x).
Axes of the slice: x: 2, y: 2, z: 4, core: 2. Of those that a mesh axis runs over, the one named last changes fastest.
Arguments:
- queries: bfloat16 [512, 8192], P('col', 'row'), may hold values from -8 to 8
- cache_keys: bfloat16 [8, 32768, 128], P(None, ('row', 'col')), may hold values from -8 to 8
- cache_values: bfloat16 [8, 32768, 128], P(None, ('row', 'col')), may hold values from -6 to 6
- stretch_keys: bfloat16 [8, 512, 128], P(None, 'col'), may hold values from -8 to 8
- stretch_values: bfloat16 [8, 512, 128], P(None, 'col'), may hold values from -6 to 6
- block_lists: int32 [4, 8, 16], replicated, may hold values from 0 to 255, as said below
- out_weight: bfloat16 [8192, 8192], P('row', 'col'), may hold values from -0.5 to 0.5
- residual: bfloat16 [512, 8192], P('row', 'col'), may hold values from -6 to 6
- norm_gain: bfloat16 [8192], P('col'), may hold values from 0.25 to 1.75
- gate_weight: bfloat16 [8192, 28672], P('col', 'row'), may hold values from -0.0625 to 0.0625
- up_weight: bfloat16 [8192, 28672], P('col', 'row'), may hold values from -0.0625 to 0.0625
- down_weight: bfloat16 [28672, 8192], P('row', 'col'), may hold values from -0.03125 to 0.03125
Outputs:
- layer_out: bfloat16 [512, 8192], P('row', 'col')
The draws below stay inside these ranges and needn't reach their ends.
Inputs may be any that keep to these rules, and one draw needn't show every extreme that they name: `block_lists`: each list names 16 different cache blocks; device k of row+col holds cache blocks k * (8) to (k + 1) * 8 - 1, and no two blocks of one list lie on the same device. Every list holds block 0 and block 255.
All inputs are finite; a program needn't handle non-finite values.
Results may differ from the reference program's by a relative error of at most 0.0085.
Values may be sent and summed in bfloat16 or wider, within the bound.
A program may use at most 128 MiB of HBM per device.

```python
import math
import jax
import jax.numpy as jnp
from jax import lax

D = 8192
FF = 28672
HEADS = 64
KV_HEADS = 8
HEAD_DIM = 128
BLK = 128
CTX_DEV = 1024
NSEL = 16
GROUP = 8
CTX = 32768
TOKENS = 512
DEVICES = 32


def draw_queries(key, part):
    shape_full = (TOKENS, HEADS, HEAD_DIM)
    base_draw = jnp.clip(jax.random.normal(jax.random.fold_in(key, 21), shape_full, jnp.float32), -8.0, 8.0)
    return base_draw.reshape(TOKENS, HEADS * HEAD_DIM).astype(jnp.bfloat16)


def draw_cache_keys(key, part):
    shape_full = (KV_HEADS, CTX, HEAD_DIM)
    drawn = jnp.clip(2.0 * jax.random.normal(jax.random.fold_in(key, 31), shape_full, jnp.float32), -8.0, 8.0)
    return drawn.astype(jnp.bfloat16)


def draw_block_lists(key, part):
    list_count = TOKENS // BLK * KV_HEADS
    per_device = CTX_DEV // BLK
    list_keys = jax.random.split(jax.random.fold_in(key, 41), list_count)

    def one_list(list_key):
        middle = jax.random.permutation(list_key, DEVICES - 2)[:NSEL - 2] + 1
        offsets = jax.random.randint(jax.random.fold_in(list_key, 1), (NSEL - 2,), 0, per_device)
        anchored = jnp.array([0, DEVICES * per_device - 1], dtype=jnp.int32)
        return jnp.concatenate([anchored, (middle * per_device + offsets).astype(jnp.int32)])
    return jax.vmap(one_list)(list_keys).reshape(TOKENS // BLK, KV_HEADS, NSEL)


def steps_of(own_key, extent, cuts, smallest, largest):
    def one(dim, shards_of):
        steps = jax.random.uniform(jax.random.fold_in(jax.random.fold_in(own_key, 6), dim), (shards_of,), jnp.float32, smallest / len(cuts), largest / len(cuts))
        return jnp.repeat(jnp.exp(steps), extent[dim] // shards_of).reshape((-1,) + (1,) * (len(extent) - dim - 1))

    gain = one(*cuts[0])
    for cut in cuts[1:]:
        gain = gain * one(*cut)
    return gain


def noise(key, dims, spread, most, pieces=(), kind=jnp.bfloat16):
    entries = jax.random.normal(key, dims, jnp.float32) * spread
    if len(pieces) > 0:
        entries = steps_of(key, dims, pieces, -0.22, 0.18) * entries
    return jnp.clip(entries, min=-most, max=most).astype(kind)


def setup_inputs(seed: int = 0) -> dict:
    keys = jax.random.split(jax.random.key(seed), 13)
    return {
        "queries": draw_queries(jax.random.fold_in(keys[12], 71), 0),
        "cache_keys": draw_cache_keys(jax.random.fold_in(keys[12], 71), 0),
        "cache_values": noise(keys[2], (KV_HEADS, CTX, HEAD_DIM), 1.0, 6.0, ((1, 32),)),
        "stretch_keys": noise(keys[3], (KV_HEADS, TOKENS, HEAD_DIM), 2.0, 8.0, ((1, 4),)),
        "stretch_values": noise(keys[4], (KV_HEADS, TOKENS, HEAD_DIM), 1.0, 6.0, ((1, 4),)),
        "block_lists": draw_block_lists(jax.random.fold_in(keys[12], 71), 0),
        "out_weight": noise(keys[6], (HEADS * HEAD_DIM, D), (HEADS * HEAD_DIM // 64) ** -0.5, 0.5, ((0, 8), (1, 4))),
        "residual": noise(keys[7], (TOKENS, D), 1.0, 6.0, ((0, 8), (1, 4))),
        "norm_gain": jnp.clip(1.0 + 0.15 * jax.random.normal(keys[8], (D,), jnp.float32), 0.25, 1.75).astype(jnp.bfloat16),
        "gate_weight": noise(keys[9], (D, FF), D ** -0.5, 0.0625, ((0, 4), (1, 8))),
        "up_weight": noise(keys[10], (D, FF), D ** -0.5, 0.0625, ((0, 4), (1, 8))),
        "down_weight": noise(keys[11], (FF, D), FF ** -0.5, 0.03125, ((0, 8), (1, 4))),
    }


def reference(queries, cache_keys, cache_values, stretch_keys, stretch_values, block_lists, out_weight, residual, norm_gain, gate_weight, up_weight, down_weight):
    scaling = 1.0 / math.sqrt(HEAD_DIM)
    query_blocks = TOKENS // BLK
    keys_blocked = cache_keys.reshape(KV_HEADS, CTX // BLK, BLK, HEAD_DIM)
    values_blocked = cache_values.reshape(KV_HEADS, CTX // BLK, BLK, HEAD_DIM)
    grouped = queries.reshape(query_blocks, BLK, KV_HEADS, GROUP, HEAD_DIM)
    row_pos = jnp.arange(BLK * GROUP, dtype=jnp.int32) // GROUP
    key_pos = jnp.arange(TOKENS, dtype=jnp.int32)

    def attend(item_index):
        block_index = item_index // KV_HEADS
        head_index = item_index % KV_HEADS
        query_rows = grouped[block_index, :, head_index].reshape(BLK * GROUP, HEAD_DIM)
        chosen = block_lists[block_index, head_index]
        far_keys = keys_blocked[head_index][chosen].reshape(NSEL * BLK, HEAD_DIM)
        far_values = values_blocked[head_index][chosen].reshape(NSEL * BLK, HEAD_DIM)
        near_keys = stretch_keys[head_index]
        near_values = stretch_values[head_index]
        far_scores = jnp.dot(query_rows, far_keys.T, preferred_element_type=jnp.float32) * scaling
        near_scores = jnp.dot(query_rows, near_keys.T, preferred_element_type=jnp.float32) * scaling
        allowed = key_pos[None, :] <= (block_index * BLK + row_pos)[:, None]
        near_scores = jnp.where(allowed, near_scores, -1e+30)
        row_top = jnp.maximum(lax.optimization_barrier(jnp.max(far_scores, axis=1)), lax.optimization_barrier(jnp.max(near_scores, axis=1)))
        far_exp = jnp.exp(far_scores - row_top[:, None])
        near_exp = jnp.where(allowed, jnp.exp(near_scores - row_top[:, None]), 0.0)
        totals = lax.optimization_barrier(jnp.sum(far_exp, axis=1)) + lax.optimization_barrier(jnp.sum(near_exp, axis=1))
        mixed_rows = jnp.dot(far_exp.astype(jnp.bfloat16), far_values, preferred_element_type=jnp.float32)
        mixed_rows = mixed_rows + jnp.dot(near_exp.astype(jnp.bfloat16), near_values, preferred_element_type=jnp.float32)
        return (mixed_rows / totals[:, None]).astype(jnp.bfloat16).reshape(BLK, GROUP * HEAD_DIM)
    outputs = lax.map(attend, jnp.arange(query_blocks * KV_HEADS, dtype=jnp.int32))
    outputs = outputs.reshape(query_blocks, KV_HEADS, BLK, GROUP * HEAD_DIM)
    attended = jnp.transpose(outputs, (0, 2, 1, 3)).reshape(TOKENS, HEADS * HEAD_DIM)
    stream = residual.astype(jnp.float32) + jnp.dot(attended, out_weight, preferred_element_type=jnp.float32)
    squares = lax.optimization_barrier(jnp.mean(stream * stream, axis=1))
    normed = (stream * lax.rsqrt(squares + 1e-05)[:, None] * norm_gain.astype(jnp.float32)).astype(jnp.bfloat16)
    gate_proj = jnp.dot(normed, gate_weight, preferred_element_type=jnp.float32)
    up_proj = jnp.dot(normed, up_weight, preferred_element_type=jnp.float32)
    hidden = (jax.nn.silu(gate_proj) * up_proj).astype(jnp.bfloat16)
    lowered = jnp.dot(hidden, down_weight, preferred_element_type=jnp.float32)
    return (stream + lowered).astype(jnp.bfloat16)
```

```python
import math

import jax
import jax.numpy as jnp
from jax import lax
from jax.sharding import PartitionSpec as P

D = 8192
KV_HEADS = 8
HEAD_DIM = 128
BLK = 128
GROUP = 8
CHUNKS = 2


def local(
    queries,
    cache_keys,
    cache_values,
    stretch_keys,
    stretch_values,
    block_lists,
    out_weight,
    residual,
    norm_gain,
    gate_weight,
    up_weight,
    down_weight,
):
    row_count = lax.axis_size("row")
    col_count = lax.axis_size("col")
    row_index = lax.axis_index("row")
    col_index = lax.axis_index("col")
    device_count = row_count * col_count
    my_index = row_index * col_count + col_index
    local_blocks = cache_keys.shape[1] // BLK
    heads_here = queries.shape[1] // HEAD_DIM
    list_length = block_lists.shape[2]
    my_group = row_index * heads_here // GROUP
    scaling = 1.0 / math.sqrt(HEAD_DIM)
    targets = jnp.arange(device_count, dtype=jnp.int32)
    target_group = targets // col_count * heads_here // GROUP
    target_lists = block_lists[targets % col_count, target_group]
    holders = target_lists // local_blocks
    matched = holders == my_index
    found_any = jnp.any(matched, axis=1)
    within = jnp.sum(jnp.where(matched, target_lists % local_blocks, 0), axis=1)
    source_rows = target_group * local_blocks + within
    flat_keys = cache_keys.reshape(KV_HEADS * local_blocks, BLK, HEAD_DIM)
    flat_values = cache_values.reshape(KV_HEADS * local_blocks, BLK, HEAD_DIM)
    outgoing = jnp.concatenate([flat_keys[source_rows], flat_values[source_rows]], axis=2)
    outgoing = jnp.where(found_any[:, None, None], outgoing, jnp.zeros_like(outgoing))
    arrived = lax.all_to_all(outgoing, ("row", "col"), split_axis=0, concat_axis=0, tiled=True)
    my_list = block_lists[col_index, my_group]
    fetched = arrived[my_list // local_blocks].reshape(list_length * BLK, 2 * HEAD_DIM)
    far_keys = fetched[:, :HEAD_DIM]
    far_values = fetched[:, HEAD_DIM:]
    query_rows = queries.reshape(BLK * heads_here, HEAD_DIM)
    far_scores = jnp.dot(query_rows, far_keys.T, preferred_element_type=jnp.float32) * scaling
    run_max = jnp.max(far_scores, axis=1)
    far_exp = jnp.exp(far_scores - run_max[:, None])
    run_sum = jnp.sum(far_exp, axis=1)
    run_acc = jnp.dot(far_exp.astype(jnp.bfloat16), far_values, preferred_element_type=jnp.float32)
    query_pos = col_index * BLK + jnp.arange(BLK * heads_here, dtype=jnp.int32) // heads_here
    own = jnp.concatenate([stretch_keys, stretch_values], axis=2)
    own = lax.dynamic_index_in_dim(own, my_group, 0, keepdims=False)
    piece = lax.all_gather(own, "col", axis=0, tiled=True)
    piece_keys = piece[:, :HEAD_DIM]
    piece_values = piece[:, HEAD_DIM:]
    scores = jnp.dot(query_rows, piece_keys.T, preferred_element_type=jnp.float32) * scaling
    key_pos = jnp.arange(piece_keys.shape[0], dtype=jnp.int32)
    allowed = key_pos[None, :] <= query_pos[:, None]
    scores = jnp.where(allowed, scores, -1e30)
    new_max = jnp.maximum(run_max, jnp.max(scores, axis=1))
    decays = jnp.exp(run_max - new_max)
    weights = jnp.where(allowed, jnp.exp(scores - new_max[:, None]), 0.0)
    new_sum = run_sum * decays + jnp.sum(weights, axis=1)
    new_acc = run_acc * decays[:, None] + jnp.dot(
        weights.astype(jnp.bfloat16), piece_values, preferred_element_type=jnp.float32
    )
    attended = (new_acc / new_sum[:, None]).astype(jnp.bfloat16).reshape(BLK, heads_here * HEAD_DIM)
    all_attended = lax.all_gather(attended, "col", axis=0, tiled=True)
    projected = lax.psum_scatter(
        jnp.dot(all_attended, out_weight, preferred_element_type=jnp.float32).astype(jnp.bfloat16),
        "row",
        scatter_dimension=0,
        tiled=True,
    )
    stream = residual.astype(jnp.float32) + projected.astype(jnp.float32)
    scaled = (stream * norm_gain.astype(jnp.float32)).astype(jnp.bfloat16)
    block_piece = lax.all_gather(scaled, "row", axis=0, tiled=True)
    own_squares = jnp.sum(stream * stream, axis=1)
    all_squares = lax.all_gather(own_squares, ("row", "col"), axis=0)
    squares = jnp.sum(all_squares.reshape(row_count, col_count, -1), axis=1).reshape(-1)
    squares = lax.dynamic_slice_in_dim(squares, col_index * BLK, BLK)
    factor = lax.rsqrt(squares / D + 1e-05)[:, None]
    hidden_width = gate_weight.shape[1]
    width = hidden_width // CHUNKS
    down_terms = jnp.zeros((block_piece.shape[0], down_weight.shape[1]), jnp.float32)
    for chunk in range(CHUNKS):
        part = slice(chunk * width, (chunk + 1) * width)
        gate_part = jnp.dot(block_piece, gate_weight[:, part], preferred_element_type=jnp.float32)
        up_part = jnp.dot(block_piece, up_weight[:, part], preferred_element_type=jnp.float32)
        partials = jnp.concatenate(
            [gate_part.astype(jnp.bfloat16), up_part.astype(jnp.bfloat16)], axis=1
        )
        summed = lax.psum_scatter(partials, "col", scatter_dimension=0, tiled=True)
        summed = summed.astype(jnp.float32) * factor
        hidden = (jax.nn.silu(summed[:, :width]) * summed[:, width:]).astype(jnp.bfloat16)
        gathered = lax.all_gather(hidden, "col", axis=0, tiled=True)
        down_terms = down_terms + jnp.dot(
            gathered, down_weight[part], preferred_element_type=jnp.float32
        )
    mlp_part = lax.psum_scatter(
        down_terms.astype(jnp.bfloat16), "row", scatter_dimension=0, tiled=True
    )
    return (stream + mlp_part.astype(jnp.float32)).astype(jnp.bfloat16)


def solution(mesh):
    in_specs = (
        P("col", "row"),
        P(None, ("row", "col"), None),
        P(None, ("row", "col"), None),
        P(None, "col", None),
        P(None, "col", None),
        P(),
        P("row", "col"),
        P("row", "col"),
        P("col"),
        P("col", "row"),
        P("col", "row"),
        P("row", "col"),
    )
    out_specs = P("row", "col")
    return jax.shard_map(local, mesh=mesh, in_specs=in_specs, out_specs=out_specs, check_vma=False)
```

```python
import functools
import math

import jax
import jax.numpy as jnp
from jax import lax
from jax.experimental import pallas as pl
from jax.experimental.pallas import tpu as pltpu
from jax.sharding import PartitionSpec as P

D = 8192
KV_HEADS = 8
HEAD_DIM = 128
BLK = 128
GROUP = 8
WIDTH = 256
SLOTS = 3
MESH = pl.DeviceIdType.MESH


def feed_forward_kernel(
    peers,
    chunks,
    pieces_ref,
    squares_ref,
    gate_ref,
    up_ref,
    down_ref,
    out_ref,
    gate_buf,
    up_buf,
    down_buf,
    part_buf,
    sums_buf,
    hidden_buf,
    square_buf,
    factor_buf,
    total,
    gate_sem,
    up_sem,
    down_sem,
    sums_send,
    sums_recv,
    hidden_send,
    hidden_recv,
    square_send,
    square_recv,
):
    me = lax.axis_index("col")
    depth = gate_ref.shape[0]

    def target(k):
        return lax.rem(me + k, peers)

    def sums_copy(j, k):
        slot = lax.rem(j, SLOTS)
        return pltpu.make_async_remote_copy(
            src_ref=part_buf.at[slot, target(k)],
            dst_ref=sums_buf.at[slot, k - 1],
            send_sem=sums_send.at[slot, k - 1],
            recv_sem=sums_recv.at[slot, k - 1],
            device_id={"col": target(k)},
            device_id_type=MESH,
        )

    def hidden_copy(j, k):
        slot = lax.rem(j, SLOTS)
        return pltpu.make_async_remote_copy(
            src_ref=hidden_buf.at[slot, 0],
            dst_ref=hidden_buf.at[slot, k],
            send_sem=hidden_send.at[slot, k - 1],
            recv_sem=hidden_recv.at[slot, k - 1],
            device_id={"col": target(k)},
            device_id_type=MESH,
        )

    def square_copy(k):
        return pltpu.make_async_remote_copy(
            src_ref=squares_ref.at[target(k)],
            dst_ref=square_buf.at[k - 1],
            send_sem=square_send.at[k - 1],
            recv_sem=square_recv.at[k - 1],
            device_id={"col": target(k)},
            device_id_type=MESH,
        )

    def columns(j):
        return pl.ds(pl.multiple_of(j * WIDTH, WIDTH), WIDTH)

    def gate_copy(j):
        slot = lax.rem(j, 2)
        return pltpu.make_async_copy(
            gate_ref.at[:, columns(j)], gate_buf.at[slot], gate_sem.at[slot]
        )

    def up_copy(j):
        slot = lax.rem(j, 2)
        return pltpu.make_async_copy(up_ref.at[:, columns(j)], up_buf.at[slot], up_sem.at[slot])

    def down_copy(j):
        slot = lax.rem(j, 2)
        return pltpu.make_async_copy(
            down_ref.at[columns(j), :], down_buf.at[slot], down_sem.at[slot]
        )

    gate_copy(0).start()
    up_copy(0).start()
    down_copy(0).start()
    barrier = pltpu.get_barrier_semaphore()
    for k in range(1, peers):
        pl.semaphore_signal(barrier, inc=1, device_id={"col": target(k)}, device_id_type=MESH)
    pl.semaphore_wait(barrier, peers - 1)
    for k in range(1, peers):
        square_copy(k).start()
    total[...] = jnp.zeros_like(total)

    def step(i, carry):
        @pl.when(i < chunks)
        def _():
            @pl.when(i + 1 < chunks)
            def _():
                gate_copy(i + 1).start()
                up_copy(i + 1).start()

            slot = lax.rem(i, SLOTS)
            for position, (copy, buf) in enumerate(((gate_copy, gate_buf), (up_copy, up_buf))):
                copy(i).wait()
                product = jnp.dot(
                    pieces_ref[:, :depth],
                    buf[lax.rem(i, 2)],
                    preferred_element_type=jnp.float32,
                ).astype(jnp.bfloat16)
                part_buf[slot, :, :, position * WIDTH : (position + 1) * WIDTH] = product.reshape(
                    peers, BLK, WIDTH
                )
            for k in range(1, peers):
                sums_copy(i, k).start()

        @pl.when(i == 1)
        def _():
            squares = squares_ref[me]
            for k in range(1, peers):
                square_copy(k).wait()
                squares = squares + square_buf[k - 1]
            factor_buf[...] = lax.rsqrt(squares / D + 1e-05)

        @pl.when((i >= 1) & (i < chunks + 1))
        def _():
            j = i - 1
            slot = lax.rem(j, SLOTS)
            summed = part_buf[slot, me].astype(jnp.float32)
            for k in range(1, peers):
                sums_copy(j, k).wait()
                summed = summed + sums_buf[slot, k - 1].astype(jnp.float32)
            summed = summed * factor_buf[:, :1]
            gate = summed[:, :WIDTH]
            hidden_buf[slot, 0] = (
                gate / (1.0 + jnp.exp(-gate)) * summed[:, WIDTH:]
            ).astype(jnp.bfloat16)
            for k in range(1, peers):
                hidden_copy(j, k).start()

        @pl.when(i >= 2)
        def _():
            j = i - 2
            slot = lax.rem(j, SLOTS)

            @pl.when(j + 1 < chunks)
            def _():
                down_copy(j + 1).start()

            down_copy(j).wait()
            for k in range(1, peers):
                hidden_copy(j, k).wait()
            gathered = hidden_buf[slot].reshape(peers * BLK, WIDTH)
            out_width = total.shape[1]
            tile = min(512, out_width)
            for start in range(0, out_width, tile):
                total[:, start : start + tile] += jnp.dot(
                    gathered,
                    down_buf[lax.rem(j, 2), :, start : start + tile],
                    preferred_element_type=jnp.float32,
                )

        return carry

    lax.fori_loop(0, chunks + 2, step, 0)
    for k in range(peers):
        owner = lax.rem(me + peers - k, peers)
        out_ref[owner] = total[k * BLK : (k + 1) * BLK, :].astype(jnp.bfloat16)


def feed_forward(pieces, squares, gate_weight, up_weight, down_weight):
    peers = lax.axis_size("col")
    depth, hidden_width = gate_weight.shape
    out_width = down_weight.shape[1]
    chunks = hidden_width // WIDTH
    vmem = pl.BlockSpec(memory_space=pltpu.VMEM)
    hbm = pl.BlockSpec(memory_space=pl.ANY)
    pair = (SLOTS, peers - 1)
    dma = pltpu.SemaphoreType.DMA
    return pl.pallas_call(
        functools.partial(feed_forward_kernel, peers, chunks),
        out_shape=jax.ShapeDtypeStruct((peers, BLK, out_width), jnp.bfloat16),
        in_specs=[vmem, vmem, hbm, hbm, hbm],
        out_specs=vmem,
        scratch_shapes=[
            pltpu.VMEM((2, depth, WIDTH), jnp.bfloat16),
            pltpu.VMEM((2, depth, WIDTH), jnp.bfloat16),
            pltpu.VMEM((2, WIDTH, out_width), jnp.bfloat16),
            pltpu.VMEM((SLOTS, peers, BLK, 2 * WIDTH), jnp.bfloat16),
            pltpu.VMEM((SLOTS, peers - 1, BLK, 2 * WIDTH), jnp.bfloat16),
            pltpu.VMEM((SLOTS, peers, BLK, WIDTH), jnp.bfloat16),
            pltpu.VMEM((peers - 1, BLK, 128), jnp.float32),
            pltpu.VMEM((BLK, 128), jnp.float32),
            pltpu.VMEM((peers * BLK, out_width), jnp.float32),
            dma((2,)),
            dma((2,)),
            dma((2,)),
            dma(pair),
            dma(pair),
            dma(pair),
            dma(pair),
            dma((peers - 1,)),
            dma((peers - 1,)),
        ],
        compiler_params=pltpu.CompilerParams(
            collective_id=0, has_side_effects=True, vmem_limit_bytes=48 * 1024 * 1024
        ),
    )(pieces, squares, gate_weight, up_weight, down_weight)


def local(
    queries,
    cache_keys,
    cache_values,
    stretch_keys,
    stretch_values,
    block_lists,
    out_weight,
    residual,
    norm_gain,
    gate_weight,
    up_weight,
    down_weight,
):
    row_count = lax.axis_size("row")
    col_count = lax.axis_size("col")
    row_index = lax.axis_index("row")
    col_index = lax.axis_index("col")
    device_count = row_count * col_count
    my_index = row_index * col_count + col_index
    local_blocks = cache_keys.shape[1] // BLK
    heads_here = queries.shape[1] // HEAD_DIM
    list_length = block_lists.shape[2]
    my_group = row_index * heads_here // GROUP
    scaling = 1.0 / math.sqrt(HEAD_DIM)
    targets = jnp.arange(device_count, dtype=jnp.int32)
    target_group = targets // col_count * heads_here // GROUP
    target_lists = block_lists[targets % col_count, target_group]
    holders = target_lists // local_blocks
    matched = holders == my_index
    found_any = jnp.any(matched, axis=1)
    within = jnp.sum(jnp.where(matched, target_lists % local_blocks, 0), axis=1)
    source_rows = target_group * local_blocks + within
    flat_keys = cache_keys.reshape(KV_HEADS * local_blocks, BLK, HEAD_DIM)
    flat_values = cache_values.reshape(KV_HEADS * local_blocks, BLK, HEAD_DIM)
    outgoing = jnp.concatenate([flat_keys[source_rows], flat_values[source_rows]], axis=2)
    outgoing = jnp.where(found_any[:, None, None], outgoing, jnp.zeros_like(outgoing))
    arrived = lax.all_to_all(outgoing, ("row", "col"), split_axis=0, concat_axis=0, tiled=True)
    my_list = block_lists[col_index, my_group]
    fetched = arrived[my_list // local_blocks].reshape(list_length * BLK, 2 * HEAD_DIM)
    far_keys = fetched[:, :HEAD_DIM]
    far_values = fetched[:, HEAD_DIM:]
    query_rows = queries.reshape(BLK * heads_here, HEAD_DIM)
    far_scores = jnp.dot(query_rows, far_keys.T, preferred_element_type=jnp.float32) * scaling
    run_max = jnp.max(far_scores, axis=1)
    far_exp = jnp.exp(far_scores - run_max[:, None])
    run_sum = jnp.sum(far_exp, axis=1)
    run_acc = jnp.dot(far_exp.astype(jnp.bfloat16), far_values, preferred_element_type=jnp.float32)
    query_pos = col_index * BLK + jnp.arange(BLK * heads_here, dtype=jnp.int32) // heads_here
    own = jnp.concatenate([stretch_keys, stretch_values], axis=2)
    own = lax.dynamic_index_in_dim(own, my_group, 0, keepdims=False)
    piece = lax.all_gather(own, "col", axis=0, tiled=True)
    piece_keys = piece[:, :HEAD_DIM]
    piece_values = piece[:, HEAD_DIM:]
    scores = jnp.dot(query_rows, piece_keys.T, preferred_element_type=jnp.float32) * scaling
    key_pos = jnp.arange(piece_keys.shape[0], dtype=jnp.int32)
    allowed = key_pos[None, :] <= query_pos[:, None]
    scores = jnp.where(allowed, scores, -1e30)
    new_max = jnp.maximum(run_max, jnp.max(scores, axis=1))
    decays = jnp.exp(run_max - new_max)
    weights = jnp.where(allowed, jnp.exp(scores - new_max[:, None]), 0.0)
    new_sum = run_sum * decays + jnp.sum(weights, axis=1)
    new_acc = run_acc * decays[:, None] + jnp.dot(
        weights.astype(jnp.bfloat16), piece_values, preferred_element_type=jnp.float32
    )
    attended = (new_acc / new_sum[:, None]).astype(jnp.bfloat16).reshape(BLK, heads_here * HEAD_DIM)
    all_attended = lax.all_gather(attended, "col", axis=0, tiled=True)
    projected = lax.psum_scatter(
        jnp.dot(all_attended, out_weight, preferred_element_type=jnp.float32).astype(jnp.bfloat16),
        "row",
        scatter_dimension=0,
        tiled=True,
    )
    stream = residual.astype(jnp.float32) + projected.astype(jnp.float32)
    scaled = (stream * norm_gain.astype(jnp.float32)).astype(jnp.bfloat16)
    rest = jnp.sum(stream * stream, axis=1, keepdims=True)
    terms = []
    for _ in range(3):
        term = lax.reduce_precision(rest, exponent_bits=8, mantissa_bits=7)
        terms.append(term)
        rest = rest - term
    riders = jnp.concatenate(terms + [jnp.zeros((rest.shape[0], 125), jnp.float32)], axis=1)
    outgoing_piece = jnp.concatenate([scaled, riders.astype(jnp.bfloat16)], axis=1)
    pieces = lax.all_gather(outgoing_piece, "row", axis=0, tiled=True)
    squares = jnp.sum(pieces[:, scaled.shape[1] :].astype(jnp.float32), axis=1, keepdims=True)
    squares = jnp.broadcast_to(squares, (squares.shape[0], 128)).reshape(col_count, BLK, 128)
    down_terms = feed_forward(pieces, squares, gate_weight, up_weight, down_weight)
    mlp_part = lax.psum_scatter(
        down_terms.reshape(-1, down_terms.shape[2]), "row", scatter_dimension=0, tiled=True
    )
    return (stream + mlp_part.astype(jnp.float32)).astype(jnp.bfloat16)


def solution(mesh):
    in_specs = (
        P("col", "row"),
        P(None, ("row", "col"), None),
        P(None, ("row", "col"), None),
        P(None, "col", None),
        P(None, "col", None),
        P(),
        P("row", "col"),
        P("row", "col"),
        P("col"),
        P("col", "row"),
        P("col", "row"),
        P("row", "col"),
    )
    out_specs = P("row", "col")
    return jax.shard_map(local, mesh=mesh, in_specs=in_specs, out_specs=out_specs, check_vma=False)
```

```python
import functools
import math

import jax
import jax.numpy as jnp
from jax import lax
from jax.experimental import pallas as pl
from jax.experimental.pallas import tpu as pltpu
from jax.sharding import PartitionSpec as P

D = 8192
KV_HEADS = 8
HEAD_DIM = 128
BLK = 128
GROUP = 8
WIDTH = 256
SLOTS = 4
MESH = pl.DeviceIdType.MESH


def feed_forward_kernel(
    peers,
    chunks,
    pieces_ref,
    squares_ref,
    gate_ref,
    up_ref,
    down_ref,
    out_ref,
    gate_buf,
    up_buf,
    down_buf,
    gate_part,
    up_part,
    gate_first,
    up_first,
    gate_mid,
    up_mid,
    gate_second,
    up_second,
    left,
    right,
    square_buf,
    factor_buf,
    total,
    gate_sem,
    up_sem,
    down_sem,
    pair_send,
    pair_recv,
    line_send,
    line_recv,
    square_send,
    square_recv,
):
    me = lax.axis_index("col")
    depth = gate_ref.shape[0]
    lines = peers // 2
    half = WIDTH // 2
    pair_me = lax.rem(me, 2)
    line_me = me // 2
    other = line_me * 2 + (1 - pair_me)

    def line(k):
        return lax.rem(line_me + k, lines)

    def remote(src, dst, send, recv, device):
        return pltpu.make_async_remote_copy(
            src_ref=src,
            dst_ref=dst,
            send_sem=send,
            recv_sem=recv,
            device_id={"col": device},
            device_id_type=MESH,
        )

    def transfers(stage, slot):
        if stage == 0:
            pair = (gate_part.at[slot, 1 - pair_me], gate_first.at[slot])
            along = [(up_part.at[slot, line(k)], up_first.at[slot, k - 1]) for k in range(1, lines)]
        elif stage == 1:
            pair = (up_mid.at[slot, 1 - pair_me], up_second.at[slot])
            along = [(gate_mid.at[slot, line(k)], gate_second.at[slot, k - 1]) for k in range(1, lines)]
        elif stage == 2:
            pair = (left.at[slot, 0, 0], left.at[slot, 0, 1])
            along = [(right.at[slot, 0, 0], right.at[slot, 0, k]) for k in range(1, lines)]
        else:
            pair = (right.at[slot, 0], right.at[slot, 1])
            along = [(left.at[slot, 0], left.at[slot, k]) for k in range(1, lines)]
        copies = [
            remote(*pair, pair_send.at[stage, slot], pair_recv.at[stage, slot], other)
        ]
        for k in range(1, lines):
            copies.append(
                remote(
                    *along[k - 1],
                    line_send.at[stage, slot, k - 1],
                    line_recv.at[stage, slot, k - 1],
                    line(k) * 2 + pair_me,
                )
            )
        return copies

    def square_copy(k):
        return remote(
            squares_ref.at[lax.rem(me + k, peers)],
            square_buf.at[k - 1],
            square_send.at[k - 1],
            square_recv.at[k - 1],
            lax.rem(me + k, peers),
        )

    def columns(j):
        return pl.ds(pl.multiple_of(j * WIDTH, WIDTH), WIDTH)

    def gate_copy(j):
        slot = lax.rem(j, 2)
        return pltpu.make_async_copy(
            gate_ref.at[:, columns(j)], gate_buf.at[slot], gate_sem.at[slot]
        )

    def up_copy(j):
        slot = lax.rem(j, 2)
        return pltpu.make_async_copy(up_ref.at[:, columns(j)], up_buf.at[slot], up_sem.at[slot])

    def down_copy(j):
        slot = lax.rem(j, 2)
        return pltpu.make_async_copy(
            down_ref.at[columns(j), :], down_buf.at[slot], down_sem.at[slot]
        )

    gate_copy(0).start()
    up_copy(0).start()
    down_copy(0).start()
    barrier = pltpu.get_barrier_semaphore()
    for k in range(1, peers):
        pl.semaphore_signal(
            barrier, inc=1, device_id={"col": lax.rem(me + k, peers)}, device_id_type=MESH
        )
    pl.semaphore_wait(barrier, peers - 1)
    for k in range(1, peers):
        square_copy(k).start()
    total[...] = jnp.zeros_like(total)

    def stage_when(i, stage):
        return pl.when((i >= stage) & (i < chunks + stage))

    def step(i, carry):
        @stage_when(i, 0)
        def _():
            @pl.when(i + 1 < chunks)
            def _():
                gate_copy(i + 1).start()
                up_copy(i + 1).start()

            slot = lax.rem(i, SLOTS)
            gate_copy(i).wait()
            product = jnp.dot(
                pieces_ref[:, :depth], gate_buf[lax.rem(i, 2)], preferred_element_type=jnp.float32
            ).astype(jnp.bfloat16)
            for b in range(peers):
                gate_part[slot, b % 2, b // 2] = product[b * BLK : (b + 1) * BLK]
            up_copy(i).wait()
            product = jnp.dot(
                pieces_ref[:, :depth], up_buf[lax.rem(i, 2)], preferred_element_type=jnp.float32
            ).astype(jnp.bfloat16)
            for b in range(peers):
                up_part[slot, b // 2, b % 2] = product[b * BLK : (b + 1) * BLK]
            for copy in transfers(0, slot):
                copy.start()

        @stage_when(i, 1)
        def _():
            slot = lax.rem(i - 1, SLOTS)
            for copy in transfers(0, slot):
                copy.wait()
            gate_mid[slot] = (
                gate_part[slot, pair_me].astype(jnp.float32) + gate_first[slot].astype(jnp.float32)
            ).astype(jnp.bfloat16)
            up_sum = up_part[slot, line_me].astype(jnp.float32)
            for k in range(1, lines):
                up_sum = up_sum + up_first[slot, k - 1].astype(jnp.float32)
            up_mid[slot] = up_sum.astype(jnp.bfloat16)
            for copy in transfers(1, slot):
                copy.start()

        @pl.when(i == 2)
        def _():
            squares = squares_ref[me]
            for k in range(1, peers):
                square_copy(k).wait()
                squares = squares + square_buf[k - 1]
            factor_buf[...] = lax.rsqrt(squares / D + 1e-05)

        @stage_when(i, 2)
        def _():
            slot = lax.rem(i - 2, SLOTS)
            for copy in transfers(1, slot):
                copy.wait()
            gate = gate_mid[slot, line_me].astype(jnp.float32)
            for k in range(1, lines):
                gate = gate + gate_second[slot, k - 1].astype(jnp.float32)
            up = up_mid[slot, pair_me].astype(jnp.float32) + up_second[slot].astype(jnp.float32)
            factor = factor_buf[:, :1]
            gate = gate * factor
            hidden = (gate / (1.0 + jnp.exp(-gate)) * (up * factor)).astype(jnp.bfloat16)
            left[slot, 0, 0] = hidden[:, :half]
            right[slot, 0, 0] = hidden[:, half:]
            for copy in transfers(2, slot):
                copy.start()

        @stage_when(i, 3)
        def _():
            slot = lax.rem(i - 3, SLOTS)
            for copy in transfers(2, slot):
                copy.wait()
            for copy in transfers(3, slot):
                copy.start()

        @stage_when(i, 4)
        def _():
            j = i - 4
            slot = lax.rem(j, SLOTS)

            @pl.when(j + 1 < chunks)
            def _():
                down_copy(j + 1).start()

            down_copy(j).wait()
            for copy in transfers(3, slot):
                copy.wait()
            gathered = jnp.concatenate(
                [
                    jnp.concatenate([left[slot, k, p], right[slot, p, k]], axis=1)
                    for p in range(2)
                    for k in range(lines)
                ],
                axis=0,
            )
            out_width = total.shape[1]
            tile = min(512, out_width)
            for start in range(0, out_width, tile):
                total[:, start : start + tile] += jnp.dot(
                    gathered,
                    down_buf[lax.rem(j, 2), :, start : start + tile],
                    preferred_element_type=jnp.float32,
                )

        return carry

    lax.fori_loop(0, chunks + 4, step, 0)
    for p in range(2):
        for k in range(lines):
            owner = line(lines - k) * 2 + lax.rem(pair_me + p, 2)
            first = (p * lines + k) * BLK
            out_ref[owner] = total[first : first + BLK, :].astype(jnp.bfloat16)


def feed_forward(pieces, squares, gate_weight, up_weight, down_weight):
    peers = lax.axis_size("col")
    lines = peers // 2
    depth, hidden_width = gate_weight.shape
    out_width = down_weight.shape[1]
    chunks = hidden_width // WIDTH
    vmem = pl.BlockSpec(memory_space=pltpu.VMEM)
    hbm = pl.BlockSpec(memory_space=pl.ANY)
    dma = pltpu.SemaphoreType.DMA

    def held(*shape):
        return pltpu.VMEM(shape, jnp.bfloat16)

    return pl.pallas_call(
        functools.partial(feed_forward_kernel, peers, chunks),
        out_shape=jax.ShapeDtypeStruct((peers, BLK, out_width), jnp.bfloat16),
        in_specs=[vmem, vmem, hbm, hbm, hbm],
        out_specs=vmem,
        scratch_shapes=[
            held(2, depth, WIDTH),
            held(2, depth, WIDTH),
            held(2, WIDTH, out_width),
            held(SLOTS, 2, lines, BLK, WIDTH),
            held(SLOTS, lines, 2, BLK, WIDTH),
            held(SLOTS, lines, BLK, WIDTH),
            held(SLOTS, lines - 1, 2, BLK, WIDTH),
            held(SLOTS, lines, BLK, WIDTH),
            held(SLOTS, 2, BLK, WIDTH),
            held(SLOTS, lines - 1, BLK, WIDTH),
            held(SLOTS, BLK, WIDTH),
            held(SLOTS, lines, 2, BLK, WIDTH // 2),
            held(SLOTS, 2, lines, BLK, WIDTH // 2),
            pltpu.VMEM((peers - 1, BLK, 128), jnp.float32),
            pltpu.VMEM((BLK, 128), jnp.float32),
            pltpu.VMEM((peers * BLK, out_width), jnp.float32),
            dma((2,)),
            dma((2,)),
            dma((2,)),
            dma((4, SLOTS)),
            dma((4, SLOTS)),
            dma((4, SLOTS, lines - 1)),
            dma((4, SLOTS, lines - 1)),
            dma((peers - 1,)),
            dma((peers - 1,)),
        ],
        compiler_params=pltpu.CompilerParams(
            collective_id=0, has_side_effects=True, vmem_limit_bytes=48 * 1024 * 1024
        ),
    )(pieces, squares, gate_weight, up_weight, down_weight)


def project_kernel(peers, own_ref, weight_ref, out_ref, gathered, weight_buf, weight_sem, send, recv):
    me = lax.axis_index("col")

    def copy_to(k):
        return pltpu.make_async_remote_copy(
            src_ref=own_ref,
            dst_ref=gathered.at[k - 1],
            send_sem=send.at[k - 1],
            recv_sem=recv.at[k - 1],
            device_id={"col": lax.rem(me + k, peers)},
            device_id_type=MESH,
        )

    weights = pltpu.make_async_copy(weight_ref, weight_buf, weight_sem)
    weights.start()
    barrier = pltpu.get_barrier_semaphore()
    for k in range(1, peers):
        pl.semaphore_signal(
            barrier, inc=1, device_id={"col": lax.rem(me + k, peers)}, device_id_type=MESH
        )
    pl.semaphore_wait(barrier, peers - 1)
    for k in range(1, peers):
        copy_to(k).start()
    weights.wait()
    out_width = weight_buf.shape[1]
    tile = min(512, out_width)
    for k in range(peers):
        if k > 0:
            copy_to(k).wait()
            rows = gathered[k - 1]
        else:
            rows = own_ref[...]
        owner = lax.rem(me + peers - k, peers)
        for start in range(0, out_width, tile):
            out_ref[owner, :, start : start + tile] = jnp.dot(
                rows, weight_buf[:, start : start + tile], preferred_element_type=jnp.float32
            ).astype(jnp.bfloat16)


def project(attended, out_weight):
    peers = lax.axis_size("col")
    width, out_width = out_weight.shape
    dma = pltpu.SemaphoreType.DMA
    return pl.pallas_call(
        functools.partial(project_kernel, peers),
        out_shape=jax.ShapeDtypeStruct((peers, BLK, out_width), jnp.bfloat16),
        in_specs=[pl.BlockSpec(memory_space=pltpu.VMEM), pl.BlockSpec(memory_space=pl.ANY)],
        out_specs=pl.BlockSpec(memory_space=pltpu.VMEM),
        scratch_shapes=[
            pltpu.VMEM((peers - 1, BLK, width), jnp.bfloat16),
            pltpu.VMEM((width, out_width), jnp.bfloat16),
            dma,
            dma((peers - 1,)),
            dma((peers - 1,)),
        ],
        compiler_params=pltpu.CompilerParams(
            collective_id=1, has_side_effects=True, vmem_limit_bytes=48 * 1024 * 1024
        ),
    )(attended, out_weight)


def local(
    queries,
    cache_keys,
    cache_values,
    stretch_keys,
    stretch_values,
    block_lists,
    out_weight,
    residual,
    norm_gain,
    gate_weight,
    up_weight,
    down_weight,
):
    row_count = lax.axis_size("row")
    col_count = lax.axis_size("col")
    row_index = lax.axis_index("row")
    col_index = lax.axis_index("col")
    device_count = row_count * col_count
    my_index = row_index * col_count + col_index
    local_blocks = cache_keys.shape[1] // BLK
    heads_here = queries.shape[1] // HEAD_DIM
    list_length = block_lists.shape[2]
    my_group = row_index * heads_here // GROUP
    scaling = 1.0 / math.sqrt(HEAD_DIM)
    targets = jnp.arange(device_count, dtype=jnp.int32)
    target_group = targets // col_count * heads_here // GROUP
    target_lists = block_lists[targets % col_count, target_group]
    holders = target_lists // local_blocks
    matched = holders == my_index
    found_any = jnp.any(matched, axis=1)
    within = jnp.sum(jnp.where(matched, target_lists % local_blocks, 0), axis=1)
    source_rows = target_group * local_blocks + within
    flat_keys = cache_keys.reshape(KV_HEADS * local_blocks, BLK, HEAD_DIM)
    flat_values = cache_values.reshape(KV_HEADS * local_blocks, BLK, HEAD_DIM)
    outgoing = jnp.concatenate([flat_keys[source_rows], flat_values[source_rows]], axis=2)
    outgoing = jnp.where(found_any[:, None, None], outgoing, jnp.zeros_like(outgoing))
    arrived = lax.all_to_all(outgoing, ("row", "col"), split_axis=0, concat_axis=0, tiled=True)
    my_list = block_lists[col_index, my_group]
    fetched = arrived[my_list // local_blocks].reshape(list_length * BLK, 2 * HEAD_DIM)
    far_keys = fetched[:, :HEAD_DIM]
    far_values = fetched[:, HEAD_DIM:]
    query_rows = queries.reshape(BLK * heads_here, HEAD_DIM)
    far_scores = jnp.dot(query_rows, far_keys.T, preferred_element_type=jnp.float32) * scaling
    run_max = jnp.max(far_scores, axis=1)
    far_exp = jnp.exp(far_scores - run_max[:, None])
    run_sum = jnp.sum(far_exp, axis=1)
    run_acc = jnp.dot(far_exp.astype(jnp.bfloat16), far_values, preferred_element_type=jnp.float32)
    query_pos = col_index * BLK + jnp.arange(BLK * heads_here, dtype=jnp.int32) // heads_here
    own = jnp.concatenate([stretch_keys, stretch_values], axis=2)
    own = lax.dynamic_index_in_dim(own, my_group, 0, keepdims=False)
    piece = lax.all_gather(own, "col", axis=0, tiled=True)
    piece_keys = piece[:, :HEAD_DIM]
    piece_values = piece[:, HEAD_DIM:]
    scores = jnp.dot(query_rows, piece_keys.T, preferred_element_type=jnp.float32) * scaling
    key_pos = jnp.arange(piece_keys.shape[0], dtype=jnp.int32)
    allowed = key_pos[None, :] <= query_pos[:, None]
    scores = jnp.where(allowed, scores, -1e30)
    new_max = jnp.maximum(run_max, jnp.max(scores, axis=1))
    decays = jnp.exp(run_max - new_max)
    weights = jnp.where(allowed, jnp.exp(scores - new_max[:, None]), 0.0)
    new_sum = run_sum * decays + jnp.sum(weights, axis=1)
    new_acc = run_acc * decays[:, None] + jnp.dot(
        weights.astype(jnp.bfloat16), piece_values, preferred_element_type=jnp.float32
    )
    attended = (new_acc / new_sum[:, None]).astype(jnp.bfloat16).reshape(BLK, heads_here * HEAD_DIM)
    projected = lax.psum_scatter(
        project(attended, out_weight).reshape(-1, out_weight.shape[1]),
        "row",
        scatter_dimension=0,
        tiled=True,
    )
    stream = residual.astype(jnp.float32) + projected.astype(jnp.float32)
    scaled = (stream * norm_gain.astype(jnp.float32)).astype(jnp.bfloat16)
    rest = jnp.sum(stream * stream, axis=1, keepdims=True)
    terms = []
    for _ in range(3):
        term = lax.reduce_precision(rest, exponent_bits=8, mantissa_bits=7)
        terms.append(term)
        rest = rest - term
    riders = jnp.concatenate(terms + [jnp.zeros((rest.shape[0], 125), jnp.float32)], axis=1)
    outgoing_piece = jnp.concatenate([scaled, riders.astype(jnp.bfloat16)], axis=1)
    pieces = lax.all_gather(outgoing_piece, "row", axis=0, tiled=True)
    squares = jnp.sum(pieces[:, scaled.shape[1] :].astype(jnp.float32), axis=1, keepdims=True)
    squares = jnp.broadcast_to(squares, (squares.shape[0], 128)).reshape(col_count, BLK, 128)
    down_terms = feed_forward(pieces, squares, gate_weight, up_weight, down_weight)
    mlp_part = lax.psum_scatter(
        down_terms.reshape(-1, down_terms.shape[2]), "row", scatter_dimension=0, tiled=True
    )
    return (stream + mlp_part.astype(jnp.float32)).astype(jnp.bfloat16)


def solution(mesh):
    in_specs = (
        P("col", "row"),
        P(None, ("row", "col"), None),
        P(None, ("row", "col"), None),
        P(None, "col", None),
        P(None, "col", None),
        P(),
        P("row", "col"),
        P("row", "col"),
        P("col"),
        P("col", "row"),
        P("col", "row"),
        P("row", "col"),
    )
    out_specs = P("row", "col")
    return jax.shard_map(local, mesh=mesh, in_specs=in_specs, out_specs=out_specs, check_vma=False)
```

```python
import functools
import math

import jax
import jax.numpy as jnp
from jax import lax
from jax.experimental import pallas as pl
from jax.experimental.pallas import tpu as pltpu
from jax.sharding import PartitionSpec as P

D = 8192
KV_HEADS = 8
HEAD_DIM = 128
BLK = 128
GROUP = 8
WIDTH = 256
SLOTS = 4
MESH = pl.DeviceIdType.MESH


def feed_forward_kernel(
    peers,
    chunks,
    pieces_ref,
    squares_ref,
    gate_ref,
    up_ref,
    down_ref,
    out_ref,
    gate_buf,
    up_buf,
    down_buf,
    gate_part,
    up_part,
    gate_first,
    up_first,
    gate_mid,
    up_mid,
    gate_second,
    up_second,
    left,
    right,
    square_buf,
    factor_buf,
    total,
    gate_sem,
    up_sem,
    down_sem,
    pair_send,
    pair_recv,
    line_send,
    line_recv,
    square_send,
    square_recv,
):
    me = lax.axis_index("col")
    depth = gate_ref.shape[0]
    lines = peers // 2
    half = WIDTH // 2
    pair_me = lax.rem(me, 2)
    line_me = me // 2
    other = line_me * 2 + (1 - pair_me)

    def line(k):
        return lax.rem(line_me + k, lines)

    def remote(src, dst, send, recv, device):
        return pltpu.make_async_remote_copy(
            src_ref=src,
            dst_ref=dst,
            send_sem=send,
            recv_sem=recv,
            device_id={"col": device},
            device_id_type=MESH,
        )

    def transfers(stage, slot):
        if stage == 0:
            pair = (gate_part.at[slot, 1 - pair_me], gate_first.at[slot])
            along = [(up_part.at[slot, line(k)], up_first.at[slot, k - 1]) for k in range(1, lines)]
        elif stage == 1:
            pair = (up_mid.at[slot, 1 - pair_me], up_second.at[slot])
            along = [(gate_mid.at[slot, line(k)], gate_second.at[slot, k - 1]) for k in range(1, lines)]
        elif stage == 2:
            pair = (left.at[slot, 0, 0], left.at[slot, 0, 1])
            along = [(right.at[slot, 0, 0], right.at[slot, 0, k]) for k in range(1, lines)]
        else:
            pair = (right.at[slot, 0], right.at[slot, 1])
            along = [(left.at[slot, 0], left.at[slot, k]) for k in range(1, lines)]
        copies = [
            remote(*pair, pair_send.at[stage, slot], pair_recv.at[stage, slot], other)
        ]
        for k in range(1, lines):
            copies.append(
                remote(
                    *along[k - 1],
                    line_send.at[stage, slot, k - 1],
                    line_recv.at[stage, slot, k - 1],
                    line(k) * 2 + pair_me,
                )
            )
        return copies

    def square_copy(k):
        return remote(
            squares_ref.at[lax.rem(me + k, peers)],
            square_buf.at[k - 1],
            square_send.at[k - 1],
            square_recv.at[k - 1],
            lax.rem(me + k, peers),
        )

    def columns(j):
        return pl.ds(pl.multiple_of(j * WIDTH, WIDTH), WIDTH)

    def gate_copy(j):
        slot = lax.rem(j, 2)
        return pltpu.make_async_copy(
            gate_ref.at[:, columns(j)], gate_buf.at[slot], gate_sem.at[slot]
        )

    def up_copy(j):
        slot = lax.rem(j, 2)
        return pltpu.make_async_copy(up_ref.at[:, columns(j)], up_buf.at[slot], up_sem.at[slot])

    def down_copy(j):
        slot = lax.rem(j, 2)
        return pltpu.make_async_copy(
            down_ref.at[columns(j), :], down_buf.at[slot], down_sem.at[slot]
        )

    gate_copy(0).start()
    up_copy(0).start()
    down_copy(0).start()
    barrier = pltpu.get_barrier_semaphore()
    for k in range(1, peers):
        pl.semaphore_signal(
            barrier, inc=1, device_id={"col": lax.rem(me + k, peers)}, device_id_type=MESH
        )
    pl.semaphore_wait(barrier, peers - 1)
    for k in range(1, peers):
        square_copy(k).start()
    total[...] = jnp.zeros_like(total)

    def stage_when(i, stage):
        return pl.when((i >= stage) & (i < chunks + stage))

    def step(i, carry):
        @stage_when(i, 0)
        def _():
            @pl.when(i + 1 < chunks)
            def _():
                gate_copy(i + 1).start()
                up_copy(i + 1).start()

            slot = lax.rem(i, SLOTS)
            gate_copy(i).wait()
            product = jnp.dot(
                pieces_ref[:, :depth], gate_buf[lax.rem(i, 2)], preferred_element_type=jnp.float32
            ).astype(jnp.bfloat16)
            for b in range(peers):
                gate_part[slot, b % 2, b // 2] = product[b * BLK : (b + 1) * BLK]
            up_copy(i).wait()
            product = jnp.dot(
                pieces_ref[:, :depth], up_buf[lax.rem(i, 2)], preferred_element_type=jnp.float32
            ).astype(jnp.bfloat16)
            for b in range(peers):
                up_part[slot, b // 2, b % 2] = product[b * BLK : (b + 1) * BLK]
            for copy in transfers(0, slot):
                copy.start()

        @stage_when(i, 1)
        def _():
            slot = lax.rem(i - 1, SLOTS)
            for copy in transfers(0, slot):
                copy.wait()
            gate_mid[slot] = (
                gate_part[slot, pair_me].astype(jnp.float32) + gate_first[slot].astype(jnp.float32)
            ).astype(jnp.bfloat16)
            up_sum = up_part[slot, line_me].astype(jnp.float32)
            for k in range(1, lines):
                up_sum = up_sum + up_first[slot, k - 1].astype(jnp.float32)
            up_mid[slot] = up_sum.astype(jnp.bfloat16)
            for copy in transfers(1, slot):
                copy.start()

        @pl.when(i == 2)
        def _():
            squares = squares_ref[me]
            for k in range(1, peers):
                square_copy(k).wait()
                squares = squares + square_buf[k - 1]
            factor_buf[...] = lax.rsqrt(squares / D + 1e-05)

        @stage_when(i, 2)
        def _():
            slot = lax.rem(i - 2, SLOTS)
            for copy in transfers(1, slot):
                copy.wait()
            gate = gate_mid[slot, line_me].astype(jnp.float32)
            for k in range(1, lines):
                gate = gate + gate_second[slot, k - 1].astype(jnp.float32)
            up = up_mid[slot, pair_me].astype(jnp.float32) + up_second[slot].astype(jnp.float32)
            factor = factor_buf[:, :1]
            gate = gate * factor
            hidden = (gate / (1.0 + jnp.exp(-gate)) * (up * factor)).astype(jnp.bfloat16)
            left[slot, 0, 0] = hidden[:, :half]
            right[slot, 0, 0] = hidden[:, half:]
            for copy in transfers(2, slot):
                copy.start()

        @stage_when(i, 3)
        def _():
            slot = lax.rem(i - 3, SLOTS)
            for copy in transfers(2, slot):
                copy.wait()
            for copy in transfers(3, slot):
                copy.start()

        @stage_when(i, 4)
        def _():
            j = i - 4
            slot = lax.rem(j, SLOTS)

            @pl.when(j + 1 < chunks)
            def _():
                down_copy(j + 1).start()

            down_copy(j).wait()
            for copy in transfers(3, slot):
                copy.wait()
            gathered = jnp.concatenate(
                [
                    jnp.concatenate([left[slot, k, p], right[slot, p, k]], axis=1)
                    for p in range(2)
                    for k in range(lines)
                ],
                axis=0,
            )
            out_width = total.shape[1]
            tile = min(512, out_width)
            for start in range(0, out_width, tile):
                total[:, start : start + tile] += jnp.dot(
                    gathered,
                    down_buf[lax.rem(j, 2), :, start : start + tile],
                    preferred_element_type=jnp.float32,
                )

        return carry

    lax.fori_loop(0, chunks + 4, step, 0)
    for p in range(2):
        for k in range(lines):
            owner = line(lines - k) * 2 + lax.rem(pair_me + p, 2)
            first = (p * lines + k) * BLK
            out_ref[owner] = total[first : first + BLK, :].astype(jnp.bfloat16)


def feed_forward(pieces, squares, gate_weight, up_weight, down_weight):
    peers = lax.axis_size("col")
    lines = peers // 2
    depth, hidden_width = gate_weight.shape
    out_width = down_weight.shape[1]
    chunks = hidden_width // WIDTH
    vmem = pl.BlockSpec(memory_space=pltpu.VMEM)
    hbm = pl.BlockSpec(memory_space=pl.ANY)
    dma = pltpu.SemaphoreType.DMA

    def held(*shape):
        return pltpu.VMEM(shape, jnp.bfloat16)

    return pl.pallas_call(
        functools.partial(feed_forward_kernel, peers, chunks),
        out_shape=jax.ShapeDtypeStruct((peers, BLK, out_width), jnp.bfloat16),
        in_specs=[vmem, vmem, hbm, hbm, hbm],
        out_specs=vmem,
        scratch_shapes=[
            held(2, depth, WIDTH),
            held(2, depth, WIDTH),
            held(2, WIDTH, out_width),
            held(SLOTS, 2, lines, BLK, WIDTH),
            held(SLOTS, lines, 2, BLK, WIDTH),
            held(SLOTS, lines, BLK, WIDTH),
            held(SLOTS, lines - 1, 2, BLK, WIDTH),
            held(SLOTS, lines, BLK, WIDTH),
            held(SLOTS, 2, BLK, WIDTH),
            held(SLOTS, lines - 1, BLK, WIDTH),
            held(SLOTS, BLK, WIDTH),
            held(SLOTS, lines, 2, BLK, WIDTH // 2),
            held(SLOTS, 2, lines, BLK, WIDTH // 2),
            pltpu.VMEM((peers - 1, BLK, 128), jnp.float32),
            pltpu.VMEM((BLK, 128), jnp.float32),
            pltpu.VMEM((peers * BLK, out_width), jnp.float32),
            dma((2,)),
            dma((2,)),
            dma((2,)),
            dma((4, SLOTS)),
            dma((4, SLOTS)),
            dma((4, SLOTS, lines - 1)),
            dma((4, SLOTS, lines - 1)),
            dma((peers - 1,)),
            dma((peers - 1,)),
        ],
        compiler_params=pltpu.CompilerParams(
            collective_id=0, has_side_effects=True, vmem_limit_bytes=48 * 1024 * 1024
        ),
    )(pieces, squares, gate_weight, up_weight, down_weight)


def project_kernel(peers, own_ref, weight_ref, out_ref, gathered, weight_buf, weight_sem, send, recv):
    me = lax.axis_index("col")

    def copy_to(k):
        return pltpu.make_async_remote_copy(
            src_ref=own_ref,
            dst_ref=gathered.at[k - 1],
            send_sem=send.at[k - 1],
            recv_sem=recv.at[k - 1],
            device_id={"col": lax.rem(me + k, peers)},
            device_id_type=MESH,
        )

    weights = pltpu.make_async_copy(weight_ref, weight_buf, weight_sem)
    weights.start()
    barrier = pltpu.get_barrier_semaphore()
    for k in range(1, peers):
        pl.semaphore_signal(
            barrier, inc=1, device_id={"col": lax.rem(me + k, peers)}, device_id_type=MESH
        )
    pl.semaphore_wait(barrier, peers - 1)
    for k in range(1, peers):
        copy_to(k).start()
    weights.wait()
    out_width = weight_buf.shape[1]
    tile = min(512, out_width)
    for k in range(peers):
        if k > 0:
            copy_to(k).wait()
            rows = gathered[k - 1]
        else:
            rows = own_ref[...]
        owner = lax.rem(me + peers - k, peers)
        for start in range(0, out_width, tile):
            out_ref[owner, :, start : start + tile] = jnp.dot(
                rows, weight_buf[:, start : start + tile], preferred_element_type=jnp.float32
            ).astype(jnp.bfloat16)


def project(attended, out_weight):
    peers = lax.axis_size("col")
    width, out_width = out_weight.shape
    dma = pltpu.SemaphoreType.DMA
    return pl.pallas_call(
        functools.partial(project_kernel, peers),
        out_shape=jax.ShapeDtypeStruct((peers, BLK, out_width), jnp.bfloat16),
        in_specs=[pl.BlockSpec(memory_space=pltpu.VMEM), pl.BlockSpec(memory_space=pl.ANY)],
        out_specs=pl.BlockSpec(memory_space=pltpu.VMEM),
        scratch_shapes=[
            pltpu.VMEM((peers - 1, BLK, width), jnp.bfloat16),
            pltpu.VMEM((width, out_width), jnp.bfloat16),
            dma,
            dma((peers - 1,)),
            dma((peers - 1,)),
        ],
        compiler_params=pltpu.CompilerParams(
            collective_id=1, has_side_effects=True, vmem_limit_bytes=48 * 1024 * 1024
        ),
    )(attended, out_weight)


def row_sum_kernel(lines, part_ref, out_ref, first, mid, second, pair_send, pair_recv, line_send, line_recv):
    me = lax.axis_index("row")
    pair_me = lax.rem(me, 2)
    line_me = me // 2
    other = line_me * 2 + (1 - pair_me)
    pieces, _, _, width = first.shape

    def line(k):
        return lax.rem(line_me + k, lines)

    def pair_copy(c):
        return pltpu.make_async_remote_copy(
            src_ref=part_ref.at[:, 1 - pair_me, :, c * width : (c + 1) * width],
            dst_ref=first.at[c],
            send_sem=pair_send.at[c],
            recv_sem=pair_recv.at[c],
            device_id={"row": other},
            device_id_type=MESH,
        )

    def line_copy(c, k):
        return pltpu.make_async_remote_copy(
            src_ref=mid.at[c, line(k)],
            dst_ref=second.at[c, k - 1],
            send_sem=line_send.at[c, k - 1],
            recv_sem=line_recv.at[c, k - 1],
            device_id={"row": line(k) * 2 + pair_me},
            device_id_type=MESH,
        )

    barrier = pltpu.get_barrier_semaphore()
    pl.semaphore_signal(barrier, inc=1, device_id={"row": other}, device_id_type=MESH)
    for k in range(1, lines):
        pl.semaphore_signal(
            barrier, inc=1, device_id={"row": line(k) * 2 + pair_me}, device_id_type=MESH
        )
    pl.semaphore_wait(barrier, lines)
    for c in range(pieces):
        pair_copy(c).start()
    for c in range(pieces):
        pair_copy(c).wait()
        own = part_ref[:, pair_me, :, c * width : (c + 1) * width]
        mid[c] = (own.astype(jnp.float32) + first[c].astype(jnp.float32)).astype(jnp.bfloat16)
        for k in range(1, lines):
            line_copy(c, k).start()
    for c in range(pieces):
        result = mid[c, line_me].astype(jnp.float32)
        for k in range(1, lines):
            line_copy(c, k).wait()
            result = result + second[c, k - 1].astype(jnp.float32)
        out_ref[:, c * width : (c + 1) * width] = result


def row_sum(partial, collective_id):
    rows = lax.axis_size("row")
    lines = rows // 2
    width = partial.shape[-1]
    tokens = partial.shape[0] * partial.shape[1] // rows
    pieces = 4
    part = width // pieces
    vmem = pl.BlockSpec(memory_space=pltpu.VMEM)
    dma = pltpu.SemaphoreType.DMA
    return pl.pallas_call(
        functools.partial(row_sum_kernel, lines),
        out_shape=jax.ShapeDtypeStruct((tokens, width), jnp.float32),
        in_specs=[vmem],
        out_specs=vmem,
        scratch_shapes=[
            pltpu.VMEM((pieces, lines, tokens, part), jnp.bfloat16),
            pltpu.VMEM((pieces, lines, tokens, part), jnp.bfloat16),
            pltpu.VMEM((pieces, lines - 1, tokens, part), jnp.bfloat16),
            dma((pieces,)),
            dma((pieces,)),
            dma((pieces, lines - 1)),
            dma((pieces, lines - 1)),
        ],
        compiler_params=pltpu.CompilerParams(
            collective_id=collective_id, has_side_effects=True, vmem_limit_bytes=32 * 1024 * 1024
        ),
    )(partial.reshape(lines, 2, tokens, width))


def local(
    queries,
    cache_keys,
    cache_values,
    stretch_keys,
    stretch_values,
    block_lists,
    out_weight,
    residual,
    norm_gain,
    gate_weight,
    up_weight,
    down_weight,
):
    row_count = lax.axis_size("row")
    col_count = lax.axis_size("col")
    row_index = lax.axis_index("row")
    col_index = lax.axis_index("col")
    device_count = row_count * col_count
    my_index = row_index * col_count + col_index
    local_blocks = cache_keys.shape[1] // BLK
    heads_here = queries.shape[1] // HEAD_DIM
    list_length = block_lists.shape[2]
    my_group = row_index * heads_here // GROUP
    scaling = 1.0 / math.sqrt(HEAD_DIM)
    targets = jnp.arange(device_count, dtype=jnp.int32)
    target_group = targets // col_count * heads_here // GROUP
    target_lists = block_lists[targets % col_count, target_group]
    holders = target_lists // local_blocks
    matched = holders == my_index
    found_any = jnp.any(matched, axis=1)
    within = jnp.sum(jnp.where(matched, target_lists % local_blocks, 0), axis=1)
    source_rows = target_group * local_blocks + within
    flat_keys = cache_keys.reshape(KV_HEADS * local_blocks, BLK, HEAD_DIM)
    flat_values = cache_values.reshape(KV_HEADS * local_blocks, BLK, HEAD_DIM)
    outgoing = jnp.concatenate([flat_keys[source_rows], flat_values[source_rows]], axis=2)
    outgoing = jnp.where(found_any[:, None, None], outgoing, jnp.zeros_like(outgoing))
    arrived = lax.all_to_all(outgoing, ("row", "col"), split_axis=0, concat_axis=0, tiled=True)
    my_list = block_lists[col_index, my_group]
    fetched = arrived[my_list // local_blocks].reshape(list_length * BLK, 2 * HEAD_DIM)
    far_keys = fetched[:, :HEAD_DIM]
    far_values = fetched[:, HEAD_DIM:]
    query_rows = queries.reshape(BLK * heads_here, HEAD_DIM)
    far_scores = jnp.dot(query_rows, far_keys.T, preferred_element_type=jnp.float32) * scaling
    run_max = jnp.max(far_scores, axis=1)
    far_exp = jnp.exp(far_scores - run_max[:, None])
    run_sum = jnp.sum(far_exp, axis=1)
    run_acc = jnp.dot(far_exp.astype(jnp.bfloat16), far_values, preferred_element_type=jnp.float32)
    query_pos = col_index * BLK + jnp.arange(BLK * heads_here, dtype=jnp.int32) // heads_here
    own = jnp.concatenate([stretch_keys, stretch_values], axis=2)
    own = lax.dynamic_index_in_dim(own, my_group, 0, keepdims=False)
    piece = lax.all_gather(own, "col", axis=0, tiled=True)
    piece_keys = piece[:, :HEAD_DIM]
    piece_values = piece[:, HEAD_DIM:]
    scores = jnp.dot(query_rows, piece_keys.T, preferred_element_type=jnp.float32) * scaling
    key_pos = jnp.arange(piece_keys.shape[0], dtype=jnp.int32)
    allowed = key_pos[None, :] <= query_pos[:, None]
    scores = jnp.where(allowed, scores, -1e30)
    new_max = jnp.maximum(run_max, jnp.max(scores, axis=1))
    decays = jnp.exp(run_max - new_max)
    weights = jnp.where(allowed, jnp.exp(scores - new_max[:, None]), 0.0)
    new_sum = run_sum * decays + jnp.sum(weights, axis=1)
    new_acc = run_acc * decays[:, None] + jnp.dot(
        weights.astype(jnp.bfloat16), piece_values, preferred_element_type=jnp.float32
    )
    attended = (new_acc / new_sum[:, None]).astype(jnp.bfloat16).reshape(BLK, heads_here * HEAD_DIM)
    projected = row_sum(project(attended, out_weight), 2)
    stream = residual.astype(jnp.float32) + projected.astype(jnp.float32)
    scaled = (stream * norm_gain.astype(jnp.float32)).astype(jnp.bfloat16)
    rest = jnp.sum(stream * stream, axis=1, keepdims=True)
    terms = []
    for _ in range(3):
        term = lax.reduce_precision(rest, exponent_bits=8, mantissa_bits=7)
        terms.append(term)
        rest = rest - term
    riders = jnp.concatenate(terms + [jnp.zeros((rest.shape[0], 125), jnp.float32)], axis=1)
    outgoing_piece = jnp.concatenate([scaled, riders.astype(jnp.bfloat16)], axis=1)
    pieces = lax.all_gather(outgoing_piece, "row", axis=0, tiled=True)
    squares = jnp.sum(pieces[:, scaled.shape[1] :].astype(jnp.float32), axis=1, keepdims=True)
    squares = jnp.broadcast_to(squares, (squares.shape[0], 128)).reshape(col_count, BLK, 128)
    down_terms = feed_forward(pieces, squares, gate_weight, up_weight, down_weight)
    mlp_part = row_sum(down_terms, 3)
    return (stream + mlp_part.astype(jnp.float32)).astype(jnp.bfloat16)


def solution(mesh):
    in_specs = (
        P("col", "row"),
        P(None, ("row", "col"), None),
        P(None, ("row", "col"), None),
        P(None, "col", None),
        P(None, "col", None),
        P(),
        P("row", "col"),
        P("row", "col"),
        P("col"),
        P("col", "row"),
        P("col", "row"),
        P("row", "col"),
    )
    out_specs = P("row", "col")
    return jax.shard_map(local, mesh=mesh, in_specs=in_specs, out_specs=out_specs, check_vma=False)
```
